32 devices in a mesh: fsdp: 4 (over y, core), ctx: 4 (over z), uly: 2 (over x).
Axes of the slice: x: 2, y: 2, z: 4, core: 2. Of those that a mesh axis runs over, the one named last changes fastest.
Arguments:
- query_states: bfloat16 [12, 384, 8192], P('fsdp', 'ctx', 'uly'), may hold values from -8 to 8
- key_projections: bfloat16 [12, 384, 1024], P('fsdp', 'ctx', 'uly'), may hold values from -8 to 8
- value_projections: bfloat16 [12, 384, 1024], P('fsdp', 'ctx', 'uly'), may hold values from -6 to 6
- layer_bias: bfloat16 [10240], P('fsdp'), may hold values from -3 to 3
- positions: int32 [12, 384], P('fsdp', 'ctx'), may hold values from 0 to 383, as said below
- rescale: float32 [2, 64], replicated, may hold values from 1 to 16
- table_index: int32 [12], P('fsdp'), may hold values from 0 to 1
Outputs:
- attended: bfloat16 [12, 384, 8192], P('fsdp', 'ctx', 'uly')
The draws below stay inside these ranges and needn't reach their ends.
Inputs may be any that keep to these rules, and one draw needn't show every extreme that they name: In each sequence the rows come in aligned runs of 48; every run holds 48 consecutive positions in increasing order, starting at a multiple of 48, and every position 0 to 383 occurs once. The order of the runs differs between sequences.
All inputs are finite; a program needn't handle non-finite values.
Results may differ from the reference program's by a relative error of at most 0.012.
Values may be sent and summed in bfloat16 or wider, within the bound.
A program may use at most 64 MiB of HBM per device.

```python
import math
import jax
import jax.numpy as jnp
from jax import lax

QUERY_HEADS = 64
KEY_VALUE_HEADS = 8
HEAD_SIZE = 128
TABLES = 2
SEQUENCE_ROWS = 384
BATCH_COUNT = 12
BLOCK = 48
BIAS_LEN = 10240


def draw_query_states(key, part):
    noise_key = jax.random.fold_in(key, 17)
    complete_shape = (BATCH_COUNT, SEQUENCE_ROWS, QUERY_HEADS, HEAD_SIZE)
    value_entries = jnp.clip(2.0 * jax.random.normal(noise_key, complete_shape, jnp.float32), -8.0, 8.0)
    return value_entries.reshape(BATCH_COUNT, SEQUENCE_ROWS, QUERY_HEADS * HEAD_SIZE).astype(jnp.bfloat16)


def draw_key_projections(key, part):
    noise_key = jax.random.fold_in(key, 23)
    complete_shape = (BATCH_COUNT, SEQUENCE_ROWS, KEY_VALUE_HEADS, HEAD_SIZE)
    value_entries = jnp.clip(jax.random.normal(noise_key, complete_shape, jnp.float32), -8.0, 8.0)
    return value_entries.reshape(BATCH_COUNT, SEQUENCE_ROWS, KEY_VALUE_HEADS * HEAD_SIZE).astype(jnp.bfloat16)


def order_of(branch_key):
    return jax.random.permutation(branch_key, SEQUENCE_ROWS // BLOCK)


def draw_positions(key, part):
    orders = jax.vmap(order_of)(jax.random.split(key, BATCH_COUNT))
    row_index = jnp.arange(SEQUENCE_ROWS)
    return (orders[:, row_index // BLOCK] * BLOCK + row_index % BLOCK).astype(jnp.int32)


def touch_ends(result, own_key, smallest, top_value):
    longest = result.shape.index(max(result.shape))
    spots = []
    for shift in (0, 1):
        where = [jax.random.randint(jax.random.fold_in(own_key, axis), (), 0, length) for axis, length in enumerate(result.shape)]
        where[longest] = (where[longest] + shift) % result.shape[longest]
        spots.append(tuple(where))
    return result.at[spots[0]].set(smallest).at[spots[1]].set(top_value)


def levels(rng, dims, shards, smallest, largest):
    def one(axis_at, blocks):
        draws = jax.random.uniform(jax.random.fold_in(jax.random.fold_in(rng, 6), axis_at), (blocks,), jnp.float32, smallest / len(shards), largest / len(shards))
        return jnp.repeat(jnp.exp(draws), dims[axis_at] // blocks).reshape((-1,) + (1,) * (len(dims) - axis_at - 1))

    level = one(*shards[0])
    for cut in shards[1:]:
        level = level * one(*cut)
    return level


def gaussian(stream_key, dims, width, limit, cuts=(), kind=jnp.bfloat16):
    factor_of = levels(stream_key, dims, cuts, -0.22, 0.18) if cuts else 1.0
    result = jax.random.normal(stream_key, dims, jnp.float32) * width * factor_of
    return jnp.minimum(jnp.maximum(result, -limit), limit).astype(kind)


def setup_inputs(seed: int = 0) -> dict:
    keys = jax.random.split(jax.random.key(seed), 8)
    return {
        "query_states": draw_query_states(jax.random.fold_in(keys[7], 71), 0),
        "key_projections": draw_key_projections(jax.random.fold_in(keys[7], 71), 0),
        "value_projections": gaussian(keys[2], (BATCH_COUNT, SEQUENCE_ROWS, KEY_VALUE_HEADS * HEAD_SIZE), 1.0, 6.0, ((0, 4), (1, 4), (2, 2))),
        "layer_bias": gaussian(keys[3], (BIAS_LEN,), 0.5, 3.0, ((0, 4),)),
        "positions": draw_positions(jax.random.fold_in(keys[7], 71), 0),
        "rescale": jnp.clip(jnp.exp(jax.random.uniform(keys[5], (TABLES, HEAD_SIZE // 2), jnp.float32, math.log(1.0), math.log(16.0))), 1.0, 16.0),
        "table_index": touch_ends(jax.random.randint(keys[6], (BATCH_COUNT,), 0, TABLES), jax.random.fold_in(keys[6], 1), 0, TABLES - 1).astype(jnp.int32),
    }


rope_base = 1000000.0
masked_value = -1e+30

def apply_rotation(states, positions, scale_factors):
    half_dim = states.shape[-1] // 2
    exponent = jnp.arange(half_dim, dtype=jnp.float32) * (2.0 / states.shape[-1])
    inverse = 1.0 / (scale_factors * jnp.power(jnp.float32(rope_base), exponent)[None, :])
    angles = positions.astype(jnp.float32)[:, :, None] * inverse[:, None, :]
    cosine = jnp.cos(angles)[:, :, None, :]
    sine_wave = jnp.sin(angles)[:, :, None, :]
    leading = states[..., :half_dim]
    trailing = states[..., half_dim:]
    return jnp.concatenate([leading * cosine - trailing * sine_wave, trailing * cosine + leading * sine_wave], axis=-1)

def attend_group(operands):
    query_rows, key_rows, value_rows, row_positions = operands
    scores = jnp.einsum('qrd,kd->rqk', query_rows.astype(jnp.float32), key_rows.astype(jnp.float32)) / math.sqrt(HEAD_SIZE)
    allowed = row_positions[None, :] <= row_positions[:, None]
    highest = lax.optimization_barrier(jnp.max(jnp.where(allowed[None], scores, masked_value), axis=-1, keepdims=True))
    weights = jnp.where(allowed[None], jnp.exp(scores - highest), 0.0)
    totals = lax.optimization_barrier(jnp.sum(weights, axis=-1))
    rounded = lax.optimization_barrier(weights.astype(jnp.bfloat16))
    weighted_blend = jnp.einsum('rqk,kd->qrd', rounded.astype(jnp.float32), value_rows.astype(jnp.float32))
    return weighted_blend / jnp.transpose(totals)[:, :, None]

def reference(query_states, key_projections, value_projections, layer_bias, positions, rescale, table_index):
    bias_terms = layer_bias.astype(jnp.float32)
    query_span_width = QUERY_HEADS * HEAD_SIZE
    key_span_width = KEY_VALUE_HEADS * HEAD_SIZE
    query_bias = bias_terms[:query_span_width].reshape(QUERY_HEADS, HEAD_SIZE)
    key_offset_bias = bias_terms[query_span_width:query_span_width + key_span_width].reshape(KEY_VALUE_HEADS, HEAD_SIZE)
    value_offset_bias = bias_terms[query_span_width + key_span_width:].reshape(KEY_VALUE_HEADS, HEAD_SIZE)
    scale_factors = rescale[table_index]
    query_rotated_rows = apply_rotation(query_states.astype(jnp.float32).reshape(BATCH_COUNT, SEQUENCE_ROWS, QUERY_HEADS, HEAD_SIZE) + query_bias, positions, scale_factors).astype(jnp.bfloat16)
    key_rotated_rows = apply_rotation(key_projections.astype(jnp.float32).reshape(BATCH_COUNT, SEQUENCE_ROWS, KEY_VALUE_HEADS, HEAD_SIZE) + key_offset_bias, positions, scale_factors).astype(jnp.bfloat16)
    value_with_bias = (value_projections.astype(jnp.float32).reshape(BATCH_COUNT, SEQUENCE_ROWS, KEY_VALUE_HEADS, HEAD_SIZE) + value_offset_bias).astype(jnp.bfloat16)
    group_fraction = QUERY_HEADS // KEY_VALUE_HEADS
    grouped_rows = query_rotated_rows.reshape(BATCH_COUNT, SEQUENCE_ROWS, KEY_VALUE_HEADS, group_fraction, HEAD_SIZE).transpose(0, 2, 1, 3, 4).reshape(BATCH_COUNT * KEY_VALUE_HEADS, SEQUENCE_ROWS, group_fraction, HEAD_SIZE)
    key_group_rows = key_rotated_rows.transpose(0, 2, 1, 3).reshape(BATCH_COUNT * KEY_VALUE_HEADS, SEQUENCE_ROWS, HEAD_SIZE)
    value_group_rows = value_with_bias.transpose(0, 2, 1, 3).reshape(BATCH_COUNT * KEY_VALUE_HEADS, SEQUENCE_ROWS, HEAD_SIZE)
    position_group_rows = jnp.broadcast_to(positions[:, None, :], (BATCH_COUNT, KEY_VALUE_HEADS, SEQUENCE_ROWS)).reshape(BATCH_COUNT * KEY_VALUE_HEADS, SEQUENCE_ROWS)
    weighted_blend = lax.map(attend_group, (grouped_rows, key_group_rows, value_group_rows, position_group_rows))
    output_rows = weighted_blend.reshape(BATCH_COUNT, KEY_VALUE_HEADS, SEQUENCE_ROWS, group_fraction, HEAD_SIZE).transpose(0, 2, 1, 3, 4).reshape(BATCH_COUNT, SEQUENCE_ROWS, QUERY_HEADS * HEAD_SIZE)
    return output_rows.astype(jnp.bfloat16)
```

```python
import functools
import math

import jax
import jax.numpy as jnp
from jax import lax
from jax.experimental import pallas as pl
from jax.experimental.pallas import tpu as pltpu
from jax.sharding import PartitionSpec as P

QUERY_HEADS = 64
KEY_VALUE_HEADS = 8
HEAD_SIZE = 128
GROUP = QUERY_HEADS // KEY_VALUE_HEADS
RUN = 48

rope_base = 1000000.0
masked_value = -1e30
MESH = pl.DeviceIdType.MESH


def sine_cosine(angle):
    turns = jnp.floor(angle * (2.0 / math.pi) + 0.5)
    r = angle - turns * 1.5703125
    r = r - turns * 4.837512969970703125e-4
    r = r - turns * 7.54978995489188216e-8
    z = r * r
    s = r + r * z * (-1.6666654611e-1 + z * (8.3321608736e-3 - z * 1.9515295891e-4))
    c = 1.0 - 0.5 * z + z * z * (
        4.166664568298827e-2 + z * (-1.388731625493765e-3 + z * 2.443315711809948e-5)
    )
    quarter = turns.astype(jnp.int32) & 3
    odd = (quarter & 1) == 1
    sine = jnp.where(odd, c, s)
    cosine = jnp.where(odd, s, c)
    sine = jnp.where(quarter >= 2, -sine, sine)
    cosine = jnp.where((quarter == 1) | (quarter == 2), -cosine, cosine)
    return sine, cosine


def kernel(
    n, nf, ahead, rows_at_once,
    table_ref, q_hbm, k_hbm, v_hbm, bias_in, pos_in, rescale_ref,
    out_hbm,
    q_buf, q_rot, kv, out_buf, cos_t, sin_t, mask_t, pos_buf, bias_buf, bias_f,
    q_sem, own_sem, send_right, send_left, recv_sem,
    pos_send, pos_recv, bias_send, bias_recv, out_sem,
):
    batch, rows, _ = q_hbm.shape
    heads_kv = k_hbm.shape[2] // HEAD_SIZE
    units = batch * heads_kv
    me = lax.axis_index("ctx")
    mf = lax.axis_index("fsdp")
    mu = lax.axis_index("uly")
    shard_rows = bias_in.shape[0]
    wide = GROUP * HEAD_SIZE

    def own_copies(u):
        b, g = u // heads_kv, u % heads_kv
        lanes = pl.ds(g * HEAD_SIZE, HEAD_SIZE)
        return (
            pltpu.make_async_copy(k_hbm.at[b, :, lanes], kv.at[me, u, 0], own_sem.at[u, 0]),
            pltpu.make_async_copy(v_hbm.at[b, :, lanes], kv.at[me, u, 1], own_sem.at[u, 1]),
        )

    for u in range(units):
        for copy in own_copies(u):
            copy.start()

    def q_copy(b):
        return pltpu.make_async_copy(q_hbm.at[b], q_buf.at[b], q_sem.at[b])

    barrier = pltpu.get_barrier_semaphore()
    for d in range(1, n):
        pl.semaphore_signal(
            barrier, inc=1, device_id={"ctx": lax.rem(me + d, n)}, device_id_type=MESH
        )
    for d in range(1, nf):
        pl.semaphore_signal(
            barrier, inc=1, device_id={"fsdp": lax.rem(mf + d, nf)}, device_id_type=MESH
        )
    for b in range(batch):
        q_copy(b).start()
    pos_buf[me] = pos_in[...]
    bias_buf[mf] = bias_in[...]
    for u in range(units):
        for copy in own_copies(u):
            copy.wait()
    pl.semaphore_wait(barrier, n - 1 + nf - 1)

    def pos_copy(d):
        return pltpu.make_async_remote_copy(
            src_ref=pos_in, dst_ref=pos_buf.at[me],
            send_sem=pos_send.at[d], recv_sem=pos_recv.at[d],
            device_id={"ctx": lax.rem(me + d, n)}, device_id_type=MESH,
        )

    def bias_copy(d):
        return pltpu.make_async_remote_copy(
            src_ref=bias_in, dst_ref=bias_buf.at[mf],
            send_sem=bias_send.at[d], recv_sem=bias_recv.at[d],
            device_id={"fsdp": lax.rem(mf + d, nf)}, device_id_type=MESH,
        )

    def to_right(shard, u):
        return pltpu.make_async_remote_copy(
            src_ref=kv.at[shard, u], dst_ref=kv.at[shard, u],
            send_sem=send_right.at[shard, u], recv_sem=recv_sem.at[shard, u],
            device_id={"ctx": lax.rem(me + 1, n)}, device_id_type=MESH,
        )

    def to_left(shard, u):
        return pltpu.make_async_remote_copy(
            src_ref=kv.at[shard, u], dst_ref=kv.at[shard, u],
            send_sem=send_left.at[shard, u], recv_sem=recv_sem.at[shard, u],
            device_id={"ctx": lax.rem(me + n - 1, n)}, device_id_type=MESH,
        )

    def send_own(u):
        @pl.when(me < n - 1)
        def _():
            to_right(me, u).start()

        @pl.when(me > 0)
        def _():
            to_left(me, u).start()

    for d in range(1, n):
        pos_copy(d).start()
    for d in range(1, nf):
        bias_copy(d).start()
    for u in range(min(ahead, units)):
        send_own(u)

    for d in range(1, nf):
        bias_copy(d).wait_recv()
    for f in range(nf):
        bias_f[f] = bias_buf[f].astype(jnp.float32)

    def bias_row(row):
        return bias_f[row // shard_rows, pl.ds(row % shard_rows, 1), :]

    for d in range(1, n):
        pos_copy(d).wait_recv()

    lane = lax.broadcasted_iota(jnp.int32, (1, HEAD_SIZE), 1)
    power = jnp.exp(
        (lane % (HEAD_SIZE // 2)).astype(jnp.float32)
        * (2.0 / HEAD_SIZE * math.log(rope_base))
    )
    low_half = lane < HEAD_SIZE // 2
    run_rows = lax.broadcasted_iota(jnp.int32, (RUN, HEAD_SIZE), 0)
    keys = n * rows
    key_lane = lax.broadcasted_iota(jnp.int32, (1, keys), 1)
    query_row = lax.broadcasted_iota(jnp.int32, (RUN, 1), 0)
    for b in range(batch):
        factors = rescale_ref[0:1, :]
        for t in range(1, rescale_ref.shape[0]):
            factors = jnp.where(table_ref[b] == t, rescale_ref[t : t + 1, :], factors)
        inverse = 1.0 / (jnp.concatenate([factors, factors], axis=1) * power)

        key_pos = key_lane % RUN
        for j in range(n):
            for piece in range(rows // RUN):
                first = pos_buf[j, b : b + 1, piece * RUN : piece * RUN + 1]
                here = key_lane // RUN == j * (rows // RUN) + piece
                key_pos = key_pos + jnp.where(here, first, 0)
                place = (run_rows + first).astype(jnp.float32)
                sine, cosine = sine_cosine(place * inverse)
                block = slice(piece * RUN, (piece + 1) * RUN)
                cos_t[b, j, block, :] = cosine
                sin_t[b, j, block, :] = jnp.where(low_half, -sine, sine)
        for piece in range(rows // RUN):
            first = pos_in[b : b + 1, piece * RUN : piece * RUN + 1]
            allowed = key_pos <= query_row + first
            mask_t[b, piece * RUN : (piece + 1) * RUN, :] = jnp.where(
                allowed, 0.0, masked_value
            )

    def rotate(x, cosine, sine):
        return x * cosine + pltpu.roll(x, HEAD_SIZE // 2, 1) * sine

    query_heads_here = heads_kv * GROUP
    for b in range(batch):
        q_copy(b).wait()

        @pl.loop(0, heads_kv)
        def _(g):
            for i in range(GROUP):
                x = q_buf[
                    b, :, pl.ds(pl.multiple_of(g * wide + i * HEAD_SIZE, HEAD_SIZE), HEAD_SIZE)
                ].astype(jnp.float32)
                x = x + bias_row(mu * query_heads_here + g * GROUP + i)
                q_rot[b * heads_kv + g, i * rows : (i + 1) * rows, :] = rotate(
                    x, cos_t[b, me], sin_t[b, me]
                ).astype(jnp.bfloat16)

    scale = math.log2(math.e) / math.sqrt(HEAD_SIZE)

    def out_copy(u):
        b, g = u // heads_kv, u % heads_kv
        return pltpu.make_async_copy(
            out_buf.at[u],
            out_hbm.at[b, :, pl.ds(pl.multiple_of(g * wide, wide), wide)],
            out_sem.at[u],
        )

    def compute(u):
        b, g = u // heads_kv, u % heads_kv
        k_bias = bias_row(QUERY_HEADS + mu * heads_kv + g)
        v_bias = bias_row(QUERY_HEADS + KEY_VALUE_HEADS + mu * heads_kv + g)
        k_parts, v_parts = [], []
        for j in range(n):
            x = kv[j, u, 0].astype(jnp.float32) + k_bias
            k_parts.append(rotate(x, cos_t[b, j], sin_t[b, j]).astype(jnp.bfloat16))
            v_parts.append((kv[j, u, 1].astype(jnp.float32) + v_bias).astype(jnp.bfloat16))
        k_all = jnp.concatenate(k_parts, axis=0)
        v_all = jnp.concatenate(v_parts, axis=0)
        mask = mask_t[b]
        heads_at_once = rows_at_once
        for i in range(0, GROUP, heads_at_once):
            q = q_rot[u, i * rows : (i + heads_at_once) * rows, :]
            s = lax.dot_general(
                q, k_all, (((1,), (1,)), ((), ())), preferred_element_type=jnp.float32
            )
            s = s.reshape(heads_at_once, rows, keys) + mask[None]
            high = jnp.max(s, axis=-1, keepdims=True)
            p = jnp.exp2((s - high) * scale)
            total = jnp.sum(p, axis=-1, keepdims=True)
            o = jnp.dot(
                p.astype(jnp.bfloat16).reshape(heads_at_once * rows, keys), v_all,
                preferred_element_type=jnp.float32,
            ).reshape(heads_at_once, rows, HEAD_SIZE)
            o = (o / total).astype(jnp.bfloat16)
            for e in range(heads_at_once):
                out_buf[u, :, (i + e) * HEAD_SIZE : (i + e + 1) * HEAD_SIZE] = o[e]
        out_copy(u).start()

    lag = n - 2

    @pl.loop(0, units + lag)
    def _(t):
        @pl.when(t + ahead < units)
        def _():
            send_own(t + ahead)

        for hop in range(1, n):
            u = t - hop + 1

            @pl.when((u >= 0) & (u < units) & (me + hop < n))
            def _():
                to_left(me + hop, u).wait_recv()

                @pl.when(me > 0)
                def _():
                    to_left(me + hop, u).start()

            @pl.when((u >= 0) & (u < units) & (me - hop >= 0))
            def _():
                to_right(me - hop, u).wait_recv()

                @pl.when(me < n - 1)
                def _():
                    to_right(me - hop, u).start()

        @pl.when(t >= lag)
        def _():
            compute(t - lag)

    @pl.loop(0, units)
    def _(u):
        out_copy(u).wait()
        for j in range(n):
            @pl.when((j <= me) & (me < n - 1))
            def _():
                to_right(j, u).wait_send()

            @pl.when((j >= me) & (me > 0))
            def _():
                to_left(j, u).wait_send()

    for d in range(1, n):
        pos_copy(d).wait_send()
    for d in range(1, nf):
        bias_copy(d).wait_send()


def on_device(n, nf, q, k, v, bias, positions, rescale, table_index):
    batch, rows, width = q.shape
    heads_kv = k.shape[2] // HEAD_SIZE
    units = batch * heads_kv
    keys = n * rows
    bias = bias.reshape(-1, HEAD_SIZE)
    any_spec = pl.BlockSpec(memory_space=pl.ANY)
    vmem = pl.BlockSpec(memory_space=pltpu.VMEM)
    dma = pltpu.SemaphoreType.DMA
    return pl.pallas_call(
        functools.partial(kernel, n, nf, 3, 4 if n <= 4 else 1),
        out_shape=jax.ShapeDtypeStruct(q.shape, jnp.bfloat16),
        in_specs=[
            pl.BlockSpec(memory_space=pltpu.SMEM), any_spec, any_spec, any_spec, vmem, vmem, vmem,
        ],
        out_specs=any_spec,
        scratch_shapes=[
            pltpu.VMEM((batch, rows, width), jnp.bfloat16),
            pltpu.VMEM((units, GROUP * rows, HEAD_SIZE), jnp.bfloat16),
            pltpu.VMEM((n, units, 2, rows, HEAD_SIZE), jnp.bfloat16),
            pltpu.VMEM((units, rows, GROUP * HEAD_SIZE), jnp.bfloat16),
            pltpu.VMEM((batch, n, rows, HEAD_SIZE), jnp.float32),
            pltpu.VMEM((batch, n, rows, HEAD_SIZE), jnp.float32),
            pltpu.VMEM((batch, rows, keys), jnp.float32),
            pltpu.VMEM((n,) + positions.shape, jnp.int32),
            pltpu.VMEM((nf,) + bias.shape, jnp.bfloat16),
            pltpu.VMEM((nf,) + bias.shape, jnp.float32),
            dma((batch,)), dma((units, 2)),
            dma((n, units)), dma((n, units)), dma((n, units)),
            dma((n,)), dma((n,)), dma((nf,)), dma((nf,)), dma((units,)),
        ],
        compiler_params=pltpu.CompilerParams(
            collective_id=0, has_side_effects=True, vmem_limit_bytes=48 * 1024 * 1024
        ),
        name="relay_attention",
    )(table_index, q, k, v, bias, positions, rescale)


def solution(mesh):
    in_specs = (
        P("fsdp", "ctx", "uly"),
        P("fsdp", "ctx", "uly"),
        P("fsdp", "ctx", "uly"),
        P("fsdp"),
        P("fsdp", "ctx"),
        P(),
        P("fsdp"),
    )
    n, nf = mesh.shape["ctx"], mesh.shape["fsdp"]
    return jax.shard_map(
        functools.partial(on_device, n, nf),
        mesh=mesh, in_specs=in_specs, out_specs=P("fsdp", "ctx", "uly"), check_vma=False,
    )
```

```python
import functools
import math

import jax
import jax.numpy as jnp
from jax import lax
from jax.experimental import pallas as pl
from jax.experimental.pallas import tpu as pltpu
from jax.sharding import PartitionSpec as P

QUERY_HEADS = 64
KEY_VALUE_HEADS = 8
HEAD_SIZE = 128
GROUP = QUERY_HEADS // KEY_VALUE_HEADS
RUN = 48

rope_base = 1000000.0
masked_value = -1e30
MESH = pl.DeviceIdType.MESH


def sine_cosine(angle):
    turns = jnp.floor(angle * (2.0 / math.pi) + 0.5)
    r = angle - turns * 1.5703125
    r = r - turns * 4.837512969970703125e-4
    r = r - turns * 7.54978995489188216e-8
    z = r * r
    s = r + r * z * (-1.6666654611e-1 + z * (8.3321608736e-3 - z * 1.9515295891e-4))
    c = 1.0 - 0.5 * z + z * z * (
        4.166664568298827e-2 + z * (-1.388731625493765e-3 + z * 2.443315711809948e-5)
    )
    quarter = turns.astype(jnp.int32) & 3
    odd = (quarter & 1) == 1
    sine = jnp.where(odd, c, s)
    cosine = jnp.where(odd, s, c)
    sine = jnp.where(quarter >= 2, -sine, sine)
    cosine = jnp.where((quarter == 1) | (quarter == 2), -cosine, cosine)
    return sine, cosine


def kernel(
    n, nf, heads_at_once,
    table_hbm, q_hbm, k_hbm, v_hbm, bias_hbm, pos_hbm, rescale_hbm,
    out_ref,
    table_ref, bias_in, pos_in, rescale_ref, small_sem,
    q_buf, q_rot, kv, cos_t, sin_t, mask_t, pos_buf, bias_buf, bias_f,
    q_sem, own_sem, send_right, send_left, recv_sem,
    pos_send, pos_recv, bias_send, bias_recv,
):
    batch, rows, _ = q_hbm.shape
    heads_kv = k_hbm.shape[2] // HEAD_SIZE
    units = batch * heads_kv
    me = lax.axis_index("ctx")
    mf = lax.axis_index("fsdp")
    mu = lax.axis_index("uly")
    shard_rows = bias_in.shape[0]
    wide = GROUP * HEAD_SIZE

    barrier = pltpu.get_barrier_semaphore()
    for d in range(1, n):
        pl.semaphore_signal(
            barrier, inc=1, device_id={"ctx": lax.rem(me + d, n)}, device_id_type=MESH
        )
    for d in range(1, nf):
        pl.semaphore_signal(
            barrier, inc=1, device_id={"fsdp": lax.rem(mf + d, nf)}, device_id_type=MESH
        )
    small = [
        pltpu.make_async_copy(source, target, small_sem.at[i])
        for i, (source, target) in enumerate(
            (
                (pos_hbm, pos_in), (bias_hbm, bias_in),
                (rescale_hbm, rescale_ref), (table_hbm, table_ref),
            )
        )
    ]
    for copy in small:
        copy.start()

    def own_copies(u):
        b, g = u // heads_kv, u % heads_kv
        lanes = pl.ds(g * HEAD_SIZE, HEAD_SIZE)
        return (
            pltpu.make_async_copy(k_hbm.at[b, :, lanes], kv.at[me, u, 0], own_sem.at[u, 0]),
            pltpu.make_async_copy(v_hbm.at[b, :, lanes], kv.at[me, u, 1], own_sem.at[u, 1]),
        )

    for u in range(units):
        for copy in own_copies(u):
            copy.start()

    def q_copy(b):
        return pltpu.make_async_copy(q_hbm.at[b], q_buf.at[b], q_sem.at[b])

    for b in range(batch):
        q_copy(b).start()
    for copy in small:
        copy.wait()
    pos_buf[me] = pos_in[...]
    bias_buf[mf] = bias_in[...]
    pl.semaphore_wait(barrier, n - 1 + nf - 1)

    def pos_copy(d):
        return pltpu.make_async_remote_copy(
            src_ref=pos_in, dst_ref=pos_buf.at[me],
            send_sem=pos_send.at[d], recv_sem=pos_recv.at[d],
            device_id={"ctx": lax.rem(me + d, n)}, device_id_type=MESH,
        )

    def bias_copy(d):
        return pltpu.make_async_remote_copy(
            src_ref=bias_in, dst_ref=bias_buf.at[mf],
            send_sem=bias_send.at[d], recv_sem=bias_recv.at[d],
            device_id={"fsdp": lax.rem(mf + d, nf)}, device_id_type=MESH,
        )

    def to_right(shard, u):
        return pltpu.make_async_remote_copy(
            src_ref=kv.at[shard, u], dst_ref=kv.at[shard, u],
            send_sem=send_right.at[shard, u], recv_sem=recv_sem.at[shard, u],
            device_id={"ctx": lax.rem(me + 1, n)}, device_id_type=MESH,
        )

    def to_left(shard, u):
        return pltpu.make_async_remote_copy(
            src_ref=kv.at[shard, u], dst_ref=kv.at[shard, u],
            send_sem=send_left.at[shard, u], recv_sem=recv_sem.at[shard, u],
            device_id={"ctx": lax.rem(me + n - 1, n)}, device_id_type=MESH,
        )

    def send_own(u):
        @pl.when(me < n - 1)
        def _():
            to_right(me, u).start()

        @pl.when(me > 0)
        def _():
            to_left(me, u).start()

    for d in range(1, n):
        pos_copy(d).start()
    for d in range(1, nf):
        bias_copy(d).start()
    for u in range(units):
        for copy in own_copies(u):
            copy.wait()
        send_own(u)

    for d in range(1, nf):
        bias_copy(d).wait_recv()
    for f in range(nf):
        bias_f[f] = bias_buf[f].astype(jnp.float32)

    def bias_row(row):
        return bias_f[row // shard_rows, pl.ds(row % shard_rows, 1), :]

    for d in range(1, n):
        pos_copy(d).wait_recv()

    lane = lax.broadcasted_iota(jnp.int32, (1, HEAD_SIZE), 1)
    power = jnp.exp(
        (lane % (HEAD_SIZE // 2)).astype(jnp.float32)
        * (2.0 / HEAD_SIZE * math.log(rope_base))
    )
    low_half = lane < HEAD_SIZE // 2
    run_rows = lax.broadcasted_iota(jnp.int32, (RUN, HEAD_SIZE), 0)
    keys = n * rows
    key_lane = lax.broadcasted_iota(jnp.int32, (1, keys), 1)
    query_row = lax.broadcasted_iota(jnp.int32, (RUN, 1), 0)
    for b in range(batch):
        factors = rescale_ref[0:1, :]
        for t in range(1, rescale_ref.shape[0]):
            factors = jnp.where(table_ref[b] == t, rescale_ref[t : t + 1, :], factors)
        inverse = 1.0 / (jnp.concatenate([factors, factors], axis=1) * power)

        key_pos = key_lane % RUN
        for j in range(n):
            for piece in range(rows // RUN):
                first = pos_buf[j, b : b + 1, piece * RUN : piece * RUN + 1]
                here = key_lane // RUN == j * (rows // RUN) + piece
                key_pos = key_pos + jnp.where(here, first, 0)
                place = (run_rows + first).astype(jnp.float32)
                sine, cosine = sine_cosine(place * inverse)
                block = slice(piece * RUN, (piece + 1) * RUN)
                cos_t[b, j, block, :] = cosine
                sin_t[b, j, block, :] = jnp.where(low_half, -sine, sine)
        for piece in range(rows // RUN):
            first = pos_in[b : b + 1, piece * RUN : piece * RUN + 1]
            allowed = key_pos <= query_row + first
            mask_t[b, piece * RUN : (piece + 1) * RUN, :] = jnp.where(
                allowed, 0.0, masked_value
            )

    def rotate(x, cosine, sine):
        return x * cosine + pltpu.roll(x, HEAD_SIZE // 2, 1) * sine

    query_heads_here = heads_kv * GROUP
    for b in range(batch):
        q_copy(b).wait()

        @pl.loop(0, heads_kv)
        def _(g):
            for i in range(GROUP):
                x = q_buf[
                    b, :, pl.ds(pl.multiple_of(g * wide + i * HEAD_SIZE, HEAD_SIZE), HEAD_SIZE)
                ].astype(jnp.float32)
                x = x + bias_row(mu * query_heads_here + g * GROUP + i)
                q_rot[b * heads_kv + g, i * rows : (i + 1) * rows, :] = rotate(
                    x, cos_t[b, me], sin_t[b, me]
                ).astype(jnp.bfloat16)

    scale = math.log2(math.e) / math.sqrt(HEAD_SIZE)

    def compute(u):
        b, g = u // heads_kv, u % heads_kv
        k_bias = bias_row(QUERY_HEADS + mu * heads_kv + g)
        v_bias = bias_row(QUERY_HEADS + KEY_VALUE_HEADS + mu * heads_kv + g)
        k_parts, v_parts = [], []
        for j in range(n):
            x = kv[j, u, 0].astype(jnp.float32) + k_bias
            k_parts.append(rotate(x, cos_t[b, j], sin_t[b, j]).astype(jnp.bfloat16))
            v_parts.append((kv[j, u, 1].astype(jnp.float32) + v_bias).astype(jnp.bfloat16))
        k_all = jnp.concatenate(k_parts, axis=0)
        v_all = jnp.concatenate(v_parts, axis=0)
        mask = mask_t[b]
        for i in range(0, GROUP, heads_at_once):
            q = q_rot[u, i * rows : (i + heads_at_once) * rows, :]
            s = lax.dot_general(
                q, k_all, (((1,), (1,)), ((), ())), preferred_element_type=jnp.float32
            )
            s = s.reshape(heads_at_once, rows, keys) + mask[None]
            high = jnp.max(s, axis=-1, keepdims=True)
            p = jnp.exp2((s - high) * scale)
            total = jnp.sum(p, axis=-1, keepdims=True)
            o = jnp.dot(
                p.astype(jnp.bfloat16).reshape(heads_at_once * rows, keys), v_all,
                preferred_element_type=jnp.float32,
            ).reshape(heads_at_once, rows, HEAD_SIZE)
            o = (o / total).astype(jnp.bfloat16)
            for e in range(heads_at_once):
                start = pl.multiple_of(g * wide + (i + e) * HEAD_SIZE, HEAD_SIZE)
                out_ref[b, :, pl.ds(start, HEAD_SIZE)] = o[e]

    lag = n - 2

    @pl.loop(0, units + lag)
    def _(t):
        for hop in range(1, n):
            u = t - hop + 1

            @pl.when((u >= 0) & (u < units) & (me + hop < n))
            def _():
                to_left(me + hop, u).wait_recv()

                @pl.when(me > 0)
                def _():
                    to_left(me + hop, u).start()

            @pl.when((u >= 0) & (u < units) & (me - hop >= 0))
            def _():
                to_right(me - hop, u).wait_recv()

                @pl.when(me < n - 1)
                def _():
                    to_right(me - hop, u).start()

        @pl.when(t >= lag)
        def _():
            compute(t - lag)

    @pl.loop(0, units)
    def _(u):
        for j in range(n):
            @pl.when((j <= me) & (me < n - 1))
            def _():
                to_right(j, u).wait_send()

            @pl.when((j >= me) & (me > 0))
            def _():
                to_left(j, u).wait_send()

    for d in range(1, n):
        pos_copy(d).wait_send()
    for d in range(1, nf):
        bias_copy(d).wait_send()


def on_device(n, nf, q, k, v, bias, positions, rescale, table_index):
    batch, rows, width = q.shape
    heads_kv = k.shape[2] // HEAD_SIZE
    units = batch * heads_kv
    keys = n * rows
    bias = bias.reshape(-1, HEAD_SIZE)
    hbm = pl.BlockSpec(memory_space=pltpu.HBM)
    dma = pltpu.SemaphoreType.DMA
    return pl.pallas_call(
        functools.partial(kernel, n, nf, 8 if n <= 4 else 1),
        out_shape=jax.ShapeDtypeStruct(q.shape, jnp.bfloat16),
        in_specs=[hbm] * 7,
        out_specs=pl.BlockSpec(memory_space=pltpu.VMEM),
        scratch_shapes=[
            pltpu.SMEM(table_index.shape, jnp.int32),
            pltpu.VMEM(bias.shape, jnp.bfloat16),
            pltpu.VMEM(positions.shape, jnp.int32),
            pltpu.VMEM(rescale.shape, jnp.float32),
            dma((4,)),
            pltpu.VMEM((batch, rows, width), jnp.bfloat16),
            pltpu.VMEM((units, GROUP * rows, HEAD_SIZE), jnp.bfloat16),
            pltpu.VMEM((n, units, 2, rows, HEAD_SIZE), jnp.bfloat16),
            pltpu.VMEM((batch, n, rows, HEAD_SIZE), jnp.float32),
            pltpu.VMEM((batch, n, rows, HEAD_SIZE), jnp.float32),
            pltpu.VMEM((batch, rows, keys), jnp.float32),
            pltpu.VMEM((n,) + positions.shape, jnp.int32),
            pltpu.VMEM((nf,) + bias.shape, jnp.bfloat16),
            pltpu.VMEM((nf,) + bias.shape, jnp.float32),
            dma((batch,)), dma((units, 2)),
            dma((n, units)), dma((n, units)), dma((n, units)),
            dma((n,)), dma((n,)), dma((nf,)), dma((nf,)),
        ],
        compiler_params=pltpu.CompilerParams(
            collective_id=0, has_side_effects=True, vmem_limit_bytes=48 * 1024 * 1024
        ),
        name="relay_attention",
    )(*(pltpu.with_memory_space_constraint(x, pltpu.HBM) for x in (table_index, q, k, v, bias, positions, rescale)))


def solution(mesh):
    in_specs = (
        P("fsdp", "ctx", "uly"),
        P("fsdp", "ctx", "uly"),
        P("fsdp", "ctx", "uly"),
        P("fsdp"),
        P("fsdp", "ctx"),
        P(),
        P("fsdp"),
    )
    n, nf = mesh.shape["ctx"], mesh.shape["fsdp"]
    return jax.shard_map(
        functools.partial(on_device, n, nf),
        mesh=mesh, in_specs=in_specs, out_specs=P("fsdp", "ctx", "uly"), check_vma=False,
    )
```

```python
import functools
import math

import jax
import jax.numpy as jnp
from jax import lax
from jax.experimental import pallas as pl
from jax.experimental.pallas import tpu as pltpu
from jax.sharding import PartitionSpec as P

QUERY_HEADS = 64
KEY_VALUE_HEADS = 8
HEAD_SIZE = 128
GROUP = QUERY_HEADS // KEY_VALUE_HEADS
RUN = 48

rope_base = 1000000.0
masked_value = -1e30
MESH = pl.DeviceIdType.MESH


def sine_cosine(angle):
    turns = jnp.floor(angle * (2.0 / math.pi) + 0.5)
    r = angle - turns * 1.5703125
    r = r - turns * 4.837512969970703125e-4
    r = r - turns * 7.54978995489188216e-8
    z = r * r
    s = r + r * z * (-1.6666654611e-1 + z * (8.3321608736e-3 - z * 1.9515295891e-4))
    c = 1.0 - 0.5 * z + z * z * (
        4.166664568298827e-2 + z * (-1.388731625493765e-3 + z * 2.443315711809948e-5)
    )
    quarter = turns.astype(jnp.int32) & 3
    odd = (quarter & 1) == 1
    sine = jnp.where(odd, c, s)
    cosine = jnp.where(odd, s, c)
    sine = jnp.where(quarter >= 2, -sine, sine)
    cosine = jnp.where((quarter == 1) | (quarter == 2), -cosine, cosine)
    return sine, cosine


def chunk_bounds(units):
    bounds, first = [], 0
    while first < units:
        size = -(-(units - first) // 3)
        bounds.append((first, size))
        first += size
    return bounds


def kernel(
    n, nf, heads_at_once,
    table_hbm, q_hbm, k_hbm, v_hbm, bias_hbm, pos_hbm, rescale_hbm,
    out_ref,
    table_ref, bias_in, pos_in, rescale_ref, small_sem,
    q_buf, q_rot, kv, cos_t, sin_t, mask_t, pos_buf, bias_buf, bias_f,
    q_sem, own_sem, send_right, send_left, recv_sem,
    pos_send, pos_recv, bias_send, bias_recv,
):
    batch, rows, _ = q_hbm.shape
    heads_kv = k_hbm.shape[2] // HEAD_SIZE
    units = batch * heads_kv
    me = lax.axis_index("ctx")
    mf = lax.axis_index("fsdp")
    mu = lax.axis_index("uly")
    shard_rows = bias_in.shape[0]
    chunks = chunk_bounds(units)
    wide = GROUP * HEAD_SIZE

    barrier = pltpu.get_barrier_semaphore()
    for d in range(1, n):
        pl.semaphore_signal(
            barrier, inc=1, device_id={"ctx": lax.rem(me + d, n)}, device_id_type=MESH
        )
    for d in range(1, nf):
        pl.semaphore_signal(
            barrier, inc=1, device_id={"fsdp": lax.rem(mf + d, nf)}, device_id_type=MESH
        )
    small = [
        pltpu.make_async_copy(source, target, small_sem.at[i])
        for i, (source, target) in enumerate(
            (
                (pos_hbm, pos_in), (bias_hbm, bias_in),
                (rescale_hbm, rescale_ref), (table_hbm, table_ref),
            )
        )
    ]
    for copy in small:
        copy.start()

    def own_copies(u):
        b, g = u // heads_kv, u % heads_kv
        lanes = pl.ds(g * HEAD_SIZE, HEAD_SIZE)
        return (
            pltpu.make_async_copy(k_hbm.at[b, :, lanes], kv.at[me, u, 0], own_sem.at[u, 0]),
            pltpu.make_async_copy(v_hbm.at[b, :, lanes], kv.at[me, u, 1], own_sem.at[u, 1]),
        )

    for u in range(units):
        for copy in own_copies(u):
            copy.start()

    def q_copy(b):
        return pltpu.make_async_copy(q_hbm.at[b], q_buf.at[b], q_sem.at[b])

    for b in range(batch):
        q_copy(b).start()
    for copy in small:
        copy.wait()
    pos_buf[me] = pos_in[...]
    bias_buf[mf] = bias_in[...]
    pl.semaphore_wait(barrier, n - 1 + nf - 1)

    def pos_copy(d):
        return pltpu.make_async_remote_copy(
            src_ref=pos_in, dst_ref=pos_buf.at[me],
            send_sem=pos_send.at[d], recv_sem=pos_recv.at[d],
            device_id={"ctx": lax.rem(me + d, n)}, device_id_type=MESH,
        )

    def bias_copy(d):
        return pltpu.make_async_remote_copy(
            src_ref=bias_in, dst_ref=bias_buf.at[mf],
            send_sem=bias_send.at[d], recv_sem=bias_recv.at[d],
            device_id={"fsdp": lax.rem(mf + d, nf)}, device_id_type=MESH,
        )

    def to_right(shard, c):
        part = pl.ds(*chunks[c])
        return pltpu.make_async_remote_copy(
            src_ref=kv.at[shard, part], dst_ref=kv.at[shard, part],
            send_sem=send_right.at[shard, c], recv_sem=recv_sem.at[shard, c],
            device_id={"ctx": lax.rem(me + 1, n)}, device_id_type=MESH,
        )

    def to_left(shard, c):
        part = pl.ds(*chunks[c])
        return pltpu.make_async_remote_copy(
            src_ref=kv.at[shard, part], dst_ref=kv.at[shard, part],
            send_sem=send_left.at[shard, c], recv_sem=recv_sem.at[shard, c],
            device_id={"ctx": lax.rem(me + n - 1, n)}, device_id_type=MESH,
        )

    def send_own(c):
        @pl.when(me < n - 1)
        def _():
            to_right(me, c).start()

        @pl.when(me > 0)
        def _():
            to_left(me, c).start()

    for d in range(1, n):
        pos_copy(d).start()
    for d in range(1, nf):
        bias_copy(d).start()
    for c, (first, size) in enumerate(chunks):
        for u in range(first, first + size):
            for copy in own_copies(u):
                copy.wait()
        send_own(c)

    for d in range(1, nf):
        bias_copy(d).wait_recv()
    for f in range(nf):
        bias_f[f] = bias_buf[f].astype(jnp.float32)

    def bias_row(row):
        return bias_f[row // shard_rows, pl.ds(row % shard_rows, 1), :]

    for d in range(1, n):
        pos_copy(d).wait_recv()

    lane = lax.broadcasted_iota(jnp.int32, (1, HEAD_SIZE), 1)
    power = jnp.exp(
        (lane % (HEAD_SIZE // 2)).astype(jnp.float32)
        * (2.0 / HEAD_SIZE * math.log(rope_base))
    )
    low_half = lane < HEAD_SIZE // 2
    run_rows = lax.broadcasted_iota(jnp.int32, (RUN, HEAD_SIZE), 0)
    keys = n * rows
    key_lane = lax.broadcasted_iota(jnp.int32, (1, keys), 1)
    query_row = lax.broadcasted_iota(jnp.int32, (RUN, 1), 0)
    for b in range(batch):
        factors = rescale_ref[0:1, :]
        for t in range(1, rescale_ref.shape[0]):
            factors = jnp.where(table_ref[b] == t, rescale_ref[t : t + 1, :], factors)
        inverse = 1.0 / (jnp.concatenate([factors, factors], axis=1) * power)

        key_pos = key_lane % RUN
        for j in range(n):
            for piece in range(rows // RUN):
                first = pos_buf[j, b : b + 1, piece * RUN : piece * RUN + 1]
                here = key_lane // RUN == j * (rows // RUN) + piece
                key_pos = key_pos + jnp.where(here, first, 0)
                place = (run_rows + first).astype(jnp.float32)
                sine, cosine = sine_cosine(place * inverse)
                block = slice(piece * RUN, (piece + 1) * RUN)
                cos_t[b, j, block, :] = cosine
                sin_t[b, j, block, :] = jnp.where(low_half, -sine, sine)
        for piece in range(rows // RUN):
            first = pos_in[b : b + 1, piece * RUN : piece * RUN + 1]
            allowed = key_pos <= query_row + first
            mask_t[b, piece * RUN : (piece + 1) * RUN, :] = jnp.where(
                allowed, 0.0, masked_value
            )

    def rotate(x, cosine, sine):
        return x * cosine + pltpu.roll(x, HEAD_SIZE // 2, 1) * sine

    query_heads_here = heads_kv * GROUP
    for b in range(batch):
        q_copy(b).wait()

        @pl.loop(0, heads_kv)
        def _(g):
            for i in range(GROUP):
                x = q_buf[
                    b, :, pl.ds(pl.multiple_of(g * wide + i * HEAD_SIZE, HEAD_SIZE), HEAD_SIZE)
                ].astype(jnp.float32)
                x = x + bias_row(mu * query_heads_here + g * GROUP + i)
                q_rot[b * heads_kv + g, i * rows : (i + 1) * rows, :] = rotate(
                    x, cos_t[b, me], sin_t[b, me]
                ).astype(jnp.bfloat16)

    scale = math.log2(math.e) / math.sqrt(HEAD_SIZE)

    def compute(u):
        b, g = u // heads_kv, u % heads_kv
        k_bias = bias_row(QUERY_HEADS + mu * heads_kv + g)
        v_bias = bias_row(QUERY_HEADS + KEY_VALUE_HEADS + mu * heads_kv + g)
        k_parts, v_parts = [], []
        for j in range(n):
            x = kv[j, u, 0].astype(jnp.float32) + k_bias
            k_parts.append(rotate(x, cos_t[b, j], sin_t[b, j]).astype(jnp.bfloat16))
            v_parts.append((kv[j, u, 1].astype(jnp.float32) + v_bias).astype(jnp.bfloat16))
        k_all = jnp.concatenate(k_parts, axis=0)
        v_all = jnp.concatenate(v_parts, axis=0)
        mask = mask_t[b]
        for i in range(0, GROUP, heads_at_once):
            q = q_rot[u, i * rows : (i + heads_at_once) * rows, :]
            s = lax.dot_general(
                q, k_all, (((1,), (1,)), ((), ())), preferred_element_type=jnp.float32
            )
            s = s.reshape(heads_at_once, rows, keys) + mask[None]
            high = jnp.max(s, axis=-1, keepdims=True)
            p = jnp.exp2((s - high) * scale)
            total = jnp.sum(p, axis=-1, keepdims=True)
            o = jnp.dot(
                p.astype(jnp.bfloat16).reshape(heads_at_once * rows, keys), v_all,
                preferred_element_type=jnp.float32,
            ).reshape(heads_at_once, rows, HEAD_SIZE)
            o = (o / total).astype(jnp.bfloat16)
            for e in range(heads_at_once):
                start = pl.multiple_of(g * wide + (i + e) * HEAD_SIZE, HEAD_SIZE)
                out_ref[b, :, pl.ds(start, HEAD_SIZE)] = o[e]

    lag = n - 2

    def relay(step):
        for hop in range(1, n):
            c = step - hop + 1
            if c < 0 or c >= len(chunks):
                continue

            @pl.when(me + hop < n)
            def _():
                to_left(me + hop, c).wait_recv()

                @pl.when(me > 0)
                def _():
                    to_left(me + hop, c).start()

            @pl.when(me - hop >= 0)
            def _():
                to_right(me - hop, c).wait_recv()

                @pl.when(me < n - 1)
                def _():
                    to_right(me - hop, c).start()

    for step in range(lag):
        relay(step)

    @pl.loop(0, units)
    def _(u):
        for c, (first, _) in enumerate(chunks):
            @pl.when(u == first)
            def _():
                relay(c + lag)

        compute(u)

    for c in range(len(chunks)):
        for j in range(n):
            @pl.when((j <= me) & (me < n - 1))
            def _():
                to_right(j, c).wait_send()

            @pl.when((j >= me) & (me > 0))
            def _():
                to_left(j, c).wait_send()

    for d in range(1, n):
        pos_copy(d).wait_send()
    for d in range(1, nf):
        bias_copy(d).wait_send()


def on_device(n, nf, q, k, v, bias, positions, rescale, table_index):
    batch, rows, width = q.shape
    heads_kv = k.shape[2] // HEAD_SIZE
    units = batch * heads_kv
    keys = n * rows
    count = len(chunk_bounds(units))
    bias = bias.reshape(-1, HEAD_SIZE)
    hbm = pl.BlockSpec(memory_space=pltpu.HBM)
    dma = pltpu.SemaphoreType.DMA
    return pl.pallas_call(
        functools.partial(kernel, n, nf, 8 if n <= 4 else 1),
        out_shape=jax.ShapeDtypeStruct(q.shape, jnp.bfloat16),
        in_specs=[hbm] * 7,
        out_specs=pl.BlockSpec(memory_space=pltpu.VMEM),
        scratch_shapes=[
            pltpu.SMEM(table_index.shape, jnp.int32),
            pltpu.VMEM(bias.shape, jnp.bfloat16),
            pltpu.VMEM(positions.shape, jnp.int32),
            pltpu.VMEM(rescale.shape, jnp.float32),
            dma((4,)),
            pltpu.VMEM((batch, rows, width), jnp.bfloat16),
            pltpu.VMEM((units, GROUP * rows, HEAD_SIZE), jnp.bfloat16),
            pltpu.VMEM((n, units, 2, rows, HEAD_SIZE), jnp.bfloat16),
            pltpu.VMEM((batch, n, rows, HEAD_SIZE), jnp.float32),
            pltpu.VMEM((batch, n, rows, HEAD_SIZE), jnp.float32),
            pltpu.VMEM((batch, rows, keys), jnp.float32),
            pltpu.VMEM((n,) + positions.shape, jnp.int32),
            pltpu.VMEM((nf,) + bias.shape, jnp.bfloat16),
            pltpu.VMEM((nf,) + bias.shape, jnp.float32),
            dma((batch,)), dma((units, 2)),
            dma((n, count)), dma((n, count)), dma((n, count)),
            dma((n,)), dma((n,)), dma((nf,)), dma((nf,)),
        ],
        compiler_params=pltpu.CompilerParams(
            collective_id=0, has_side_effects=True, vmem_limit_bytes=48 * 1024 * 1024
        ),
        name="relay_attention",
    )(*(pltpu.with_memory_space_constraint(x, pltpu.HBM) for x in (table_index, q, k, v, bias, positions, rescale)))


def solution(mesh):
    in_specs = (
        P("fsdp", "ctx", "uly"),
        P("fsdp", "ctx", "uly"),
        P("fsdp", "ctx", "uly"),
        P("fsdp"),
        P("fsdp", "ctx"),
        P(),
        P("fsdp"),
    )
    n, nf = mesh.shape["ctx"], mesh.shape["fsdp"]
    return jax.shard_map(
        functools.partial(on_device, n, nf),
        mesh=mesh, in_specs=in_specs, out_specs=P("fsdp", "ctx", "uly"), check_vma=False,
    )
```
